32 devices in a mesh: wide: 8 (over y, x, core), narrow: 4 (over z).
Axes of the slice: x: 2, y: 2, z: 4, core: 2. Of those that a mesh axis runs over, the one named last changes fastest.
Arguments:
- tokens: bfloat16 [32, 1536, 768], P(('wide', 'narrow')), may hold values from -6 to 6
- lengths: int32 [8, 4], P('wide'), may hold values from 1 to 1536, 4608 in all within a row
- qkv_weight: bfloat16 [768, 3, 768], P(None, None, 'narrow'), may hold values from -0.3125 to 0.3125
- qkv_bias: bfloat16 [3, 768], P(None, 'narrow'), may hold values from -3 to 3
- out_weight: bfloat16 [768, 768], P('narrow'), may hold values from -2.5 to 2.5
- out_bias: bfloat16 [768], replicated, may hold values from -2 to 2
- norm1_gain: bfloat16 [768], replicated, may hold values from 0.099609375 to 1.8984375
- norm1_shift: bfloat16 [768], replicated, may hold values from -2 to 2
- up_weight: bfloat16 [768, 3072], P(None, 'narrow'), may hold values from -0.21875 to 0.21875
- up_bias: bfloat16 [3072], P('narrow'), may hold values from -2 to 2
- down_weight: bfloat16 [3072, 768], P('narrow'), may hold values from -0.109375 to 0.109375
- down_bias: bfloat16 [768], replicated, may hold values from -2 to 2
- norm2_gain: bfloat16 [768], replicated, may hold values from 0.099609375 to 1.8984375
- norm2_shift: bfloat16 [768], replicated, may hold values from -2 to 2
- cotangent: bfloat16 [32, 1536, 768], P(('wide', 'narrow')), may hold values from -6 to 6
Outputs:
- output: bfloat16 [32, 1536, 768], P(('wide', 'narrow'))
- input_grad: float32 [32, 1536, 768], P(('wide', 'narrow'))
- grad_qkv_weight: float32 [768, 3, 768], P(None, None, 'narrow')
- grad_qkv_bias: float32 [3, 768], P(None, 'narrow')
- grad_out_weight: float32 [768, 768], P('narrow')
- grad_out_bias: float32 [768], replicated
- grad_norm1_gain: float32 [768], replicated
- grad_norm1_shift: float32 [768], replicated
- grad_up_weight: float32 [768, 3072], P(None, 'narrow')
- grad_up_bias: float32 [3072], P('narrow')
- grad_down_weight: float32 [3072, 768], P('narrow')
- grad_down_bias: float32 [768], replicated
- grad_norm2_gain: float32 [768], replicated
- grad_norm2_shift: float32 [768], replicated
The draws below stay inside these ranges and needn't reach their ends.
Inputs may be any that keep to these rules, and one draw needn't show every extreme that they name: The 4 lengths of each wide index sum to 4608; positions at or beyond a slot's length are keys that no query attends to.
All inputs are finite; a program needn't handle non-finite values.
Results may differ from the reference program's by a relative error of at most 0.018.
The reference program's roundings to bfloat16 on the way count: a program that leaves them out, or rounds other values in their place, can miss the bound.
Values may be sent and summed in bfloat16 or wider, within the bound.
No kernel may reach another device: no remote copies, remote signals or barrier semaphores. Data moves between devices by JAX's collectives and lax.ppermute only.
A program may use at most 256 MiB of HBM per device.

```python
import math
import jax
import jax.numpy as jnp
import numpy as np
from jax import lax

D = 768
HEADS = 12
HD = 64
FF = 3072
CAP = 1536
SLOTS = 4
BATCH = 32
N_WIDE = 8


def steps_of(rng, shape, split, low, high):
    gain = 1.0
    for axis_at, shards_of in split:
        heights = jax.random.uniform(jax.random.fold_in(jax.random.fold_in(rng, 6), axis_at), (shards_of,), jnp.float32, low / len(split), high / len(split))
        gain = gain * jnp.repeat(jnp.exp(heights), shape[axis_at] // shards_of).reshape((-1,) + (1,) * (len(shape) - 1 - axis_at))
    return gain


def split_up(count, total, limit, lean):
    portions = [(1 << 20) // math.isqrt(rank ** lean) + 1 for rank in range(2, count + 1)]
    surplus, given = total - limit - (count - 1), [1] * (count - 1)
    while surplus > 0:
        movable = [i for i in range(count - 1) if given[i] < limit]
        whole, budget = sum([portions[i] for i in movable]), surplus
        for i in movable:
            extra = min(limit - given[i], max(1, budget * portions[i] // whole), surplus)
            given[i] = given[i] + extra
            surplus = surplus - extra
    return np.array([limit] + given)


def ragged_sizes(own_key, amount, total, limit, slope):
    if amount == 2:
        one = jax.random.randint(own_key, (), max(1, total - limit), min(limit, total - 1) + 1)
        return jnp.stack([one, total - one])
    tallies = jnp.asarray(split_up(amount, total, limit, slope), jnp.int32)
    pairs = (amount - 1) // 2
    source_of, receiver = tallies[1:1 + 2 * pairs:2], tallies[2:2 + 2 * pairs:2]
    slack = jnp.minimum(source_of - 1, limit - receiver)
    shifted = jax.random.randint(jax.random.fold_in(own_key, 1), (pairs,), 0, 1 << 20) % (slack + 1)
    tallies = tallies.at[1:1 + 2 * pairs:2].set(source_of - shifted).at[2:2 + 2 * pairs:2].set(receiver + shifted)
    return tallies[jax.random.permutation(jax.random.fold_in(own_key, 2), amount)]


def bell_draw(key, extent, scale, limit, shards=(), held_as=jnp.bfloat16):
    values = scale * jax.random.normal(key, extent, jnp.float32)
    if shards:
        values = values * steps_of(key, extent, shards, -0.22, 0.18)
    return jnp.clip(values, -limit, limit).astype(held_as)


def setup_inputs(seed: int = 0) -> dict:
    key_list = jax.random.split(jax.random.key(seed), 16)
    tokens = bell_draw(key_list[0], (BATCH, CAP, D), 1.0, 6.0, ((0, 32),))
    lengths = jax.vmap(lambda own: ragged_sizes(own, SLOTS, SLOTS * CAP * 3 // 4, CAP, 2))(jax.random.split(key_list[1], N_WIDE)).reshape((N_WIDE, SLOTS)).astype(jnp.int32)
    qkv_weight = bell_draw(key_list[2], (D, 3, D), (D // 2) ** -0.5, 0.3125, ((2, 4),))
    qkv_bias = bell_draw(key_list[3], (3, D), 0.5, 3.0, ((1, 4),))
    out_weight = bell_draw(key_list[4], (D, D), (max(D // 128, 1)) ** -0.5, 2.5, ((0, 4),))
    out_bias = bell_draw(key_list[5], (D,), 0.3, 2.0)
    norm1_gain = jnp.clip(1.0 + 0.18 * jax.random.normal(key_list[6], (D,), jnp.float32), 0.099609375, 1.8984375).astype(jnp.bfloat16)
    norm1_shift = bell_draw(key_list[7], (D,), 0.3, 2.0)
    up_weight = bell_draw(key_list[8], (D, FF), D ** -0.5, 0.21875, ((1, 4),))
    up_bias = bell_draw(key_list[9], (FF,), 0.3, 2.0, ((0, 4),))
    down_weight = bell_draw(key_list[10], (FF, D), FF ** -0.5, 0.109375, ((0, 4),))
    down_bias = bell_draw(key_list[11], (D,), 0.3, 2.0)
    norm2_gain = jnp.clip(1.0 + 0.18 * jax.random.normal(key_list[12], (D,), jnp.float32), 0.099609375, 1.8984375).astype(jnp.bfloat16)
    norm2_shift = bell_draw(key_list[13], (D,), 0.3, 2.0)
    cotangent = bell_draw(key_list[14], (BATCH, CAP, D), 1.0, 6.0, ((0, 32),))
    return dict(tokens=tokens, lengths=lengths, qkv_weight=qkv_weight, qkv_bias=qkv_bias, out_weight=out_weight, out_bias=out_bias, norm1_gain=norm1_gain, norm1_shift=norm1_shift, up_weight=up_weight, up_bias=up_bias, down_weight=down_weight, down_bias=down_bias, norm2_gain=norm2_gain, norm2_shift=norm2_shift, cotangent=cotangent)


@jax.custom_vjp
def low(v):
    return lax.optimization_barrier(v.astype(jnp.bfloat16)).astype(jnp.float32)

@jax.custom_vjp
def low_back(v):
    return v

def low_keep(v):
    return (low(v), None)

def low_pass(kept, grad):
    return (grad,)

def back_keep(v):
    return (v, None)

def back_low(kept, grad):
    return (low(grad),)
low.defvjp(low_keep, low_pass)
low_back.defvjp(back_keep, back_low)
FULL_PRECISION = lax.Precision.HIGHEST
NORM_EPS = 1e-06
MASK_VALUE = -1000000000.0

def matmul(left, right):
    return jnp.dot(left, right, precision=FULL_PRECISION, preferred_element_type=jnp.float32)

def layer_norm(values, gain_vec, shift_vec):
    row_mean = lax.optimization_barrier(jnp.mean(values, axis=-1, keepdims=True))
    centred = values - row_mean
    inv_std = lax.rsqrt(lax.optimization_barrier(jnp.mean(centred * centred, axis=-1, keepdims=True)) + NORM_EPS)
    return centred * inv_std * gain_vec + shift_vec

def rotate(values, cosine, sine):
    half_dim = values.shape[-1] // 2
    first_half = values[..., :half_dim]
    second_half = values[..., half_dim:]
    return jnp.concatenate([first_half * cosine - second_half * sine, second_half * cosine + first_half * sine], axis=-1)

def rotary_tables(capacity, head_dim):
    positions = jnp.arange(capacity).astype(jnp.float32)
    frequencies = 10000.0 ** (-2.0 * jnp.arange(head_dim // 2).astype(jnp.float32) / head_dim)
    angles = positions[:, None] * frequencies[None, :]
    return (jnp.cos(angles)[:, None, :], jnp.sin(angles)[:, None, :])

def layer(params, slot_tokens, slot_length):
    qkv_weight, qkv_bias, out_weight, out_bias, norm1_gain, norm1_shift, up_weight, up_bias, down_weight, down_bias, norm2_gain, norm2_shift = params
    capacity = slot_tokens.shape[0]
    projected = low_back(jnp.einsum('cd,dje->cje', slot_tokens, qkv_weight, precision=FULL_PRECISION)) + qkv_bias
    cosine, sine = rotary_tables(capacity, HD)
    queries = low(rotate(projected[:, 0].reshape(capacity, HEADS, HD), cosine, sine))
    key_rows = low(rotate(projected[:, 1].reshape(capacity, HEADS, HD), cosine, sine))
    value_rows = low(projected[:, 2].reshape(capacity, HEADS, HD))
    scores = jnp.einsum('qhe,khe->hqk', queries, key_rows, precision=FULL_PRECISION) * HD ** (-0.5)
    live_keys = jnp.arange(capacity) < slot_length
    scores = low_back(jnp.where(live_keys[None, None, :], scores, MASK_VALUE))
    row_max = lax.optimization_barrier(jnp.max(scores, axis=-1, keepdims=True))
    exponentials = jnp.exp(scores - row_max)
    weights = low(exponentials / lax.optimization_barrier(jnp.sum(exponentials, axis=-1, keepdims=True)))
    context = jnp.einsum('hqk,khe->qhe', weights, value_rows, precision=FULL_PRECISION).reshape(capacity, D)
    context = low_back(low(context))
    attended = low_back(matmul(context, out_weight)) + out_bias
    hidden = layer_norm(slot_tokens + attended, norm1_gain, norm1_shift)
    upward = low_back(matmul(low(hidden), up_weight)) + up_bias
    active = low(jax.nn.gelu(upward, approximate=False))
    downward = low_back(matmul(active, down_weight)) + down_bias
    return layer_norm(hidden + downward, norm2_gain, norm2_shift)

def reference(tokens, lengths, qkv_weight, qkv_bias, out_weight, out_bias, norm1_gain, norm1_shift, up_weight, up_bias, down_weight, down_bias, norm2_gain, norm2_shift, cotangent):
    params = tuple((argument.astype(jnp.float32) for argument in (qkv_weight, qkv_bias, out_weight, out_bias, norm1_gain, norm1_shift, up_weight, up_bias, down_weight, down_bias, norm2_gain, norm2_shift)))
    slot_lengths = lengths.reshape(-1)

    def one_slot(totals, inputs):
        slot_tokens, slot_length, slot_cotangent = inputs

        def forward(layer_params, layer_input):
            return layer(layer_params, layer_input, slot_length)
        result, pullback = jax.vjp(forward, params, slot_tokens.astype(jnp.float32))
        param_grads, input_grad = pullback(slot_cotangent.astype(jnp.float32))
        totals = jax.tree.map(jnp.add, totals, param_grads)
        return (totals, (result.astype(jnp.bfloat16), input_grad))
    zero_grads = jax.tree.map(jnp.zeros_like, params)
    totals, (output, input_grad) = lax.scan(one_slot, zero_grads, (tokens, slot_lengths, cotangent))
    return (output, input_grad, totals[0], totals[1], totals[2], totals[3], totals[4], totals[5], totals[6], totals[7], totals[8], totals[9], totals[10], totals[11])
```

```python
import jax
import jax.numpy as jnp
from jax import lax
from jax.experimental import pallas as pl
from jax.experimental.pallas import tpu as pltpu
from jax.sharding import PartitionSpec as P

HEADS = 12
HD = 64
NORM_EPS = 1e-06
MASK_VALUE = -1000000000.0
BF = jnp.bfloat16
F32 = jnp.float32
LANES = 128
VMEM_BYTES = 60 * 1024 * 1024


def nt(left, right):
    return lax.dot_general(left, right, (((1,), (1,)), ((), ())), preferred_element_type=F32)


def nn(left, right):
    return lax.dot_general(left, right, (((1,), (0,)), ((), ())), preferred_element_type=F32)


def rotary_tables(capacity, head_dim):
    positions = jnp.arange(capacity).astype(F32)
    frequencies = 10000.0 ** (-2.0 * jnp.arange(head_dim // 2).astype(F32) / head_dim)
    angles = positions[:, None] * frequencies[None, :]
    cosine = jnp.cos(angles)
    sine = jnp.sin(angles)
    reps = LANES // head_dim
    return (
        jnp.tile(jnp.concatenate([cosine, cosine], axis=1), (1, reps)),
        jnp.tile(jnp.concatenate([-sine, sine], axis=1), (1, reps)),
    )


def swap_halves(values):
    half = HD // 2
    lane = lax.broadcasted_iota(jnp.int32, values.shape, 1)
    up = pltpu.roll(values, LANES - half, 1)
    down = pltpu.roll(values, half, 1)
    return jnp.where(lane % HD < half, up, down)


def qkv_body(tok_ref, w_ref, b_ref, cos_ref, sin_ref, out_ref):
    features = tok_ref.shape[1]
    tok = tok_ref[...]
    cosine = cos_ref[...]
    sine = sin_ref[...]
    for j in range(3):
        part = nt(tok, w_ref[j * features : (j + 1) * features, :])
        part = part + b_ref[0:1, j * features : (j + 1) * features]
        for p in range(features // LANES):
            piece = part[:, p * LANES : (p + 1) * LANES]
            if j < 2:
                piece = piece * cosine + swap_halves(piece) * sine
            start = j * features + p * LANES
            out_ref[:, start : start + LANES] = piece.astype(BF)


def qkv_project(tokens, weight_t, bias, cosine, sine, block):
    rows, features = tokens.shape
    width = weight_t.shape[0]
    return pl.pallas_call(
        qkv_body,
        name="qkv",
        grid=(rows // block,),
        in_specs=[
            pl.BlockSpec((block, features), lambda i: (i, 0)),
            pl.BlockSpec((width, features), lambda i: (0, 0), pipeline_mode=pl.Buffered(1)),
            pl.BlockSpec((1, width), lambda i: (0, 0)),
            pl.BlockSpec((block, LANES), lambda i: (i, 0)),
            pl.BlockSpec((block, LANES), lambda i: (i, 0)),
        ],
        out_specs=pl.BlockSpec((block, width), lambda i: (i, 0)),
        out_shape=jax.ShapeDtypeStruct((rows, width), BF),
        compiler_params=pltpu.CompilerParams(vmem_limit_bytes=VMEM_BYTES),
    )(tokens, weight_t, bias, cosine, sine)


def head_of_lane(shape):
    return lax.broadcasted_iota(jnp.int32, shape, 1) // HD


def key_with_mask(kaug_ref, k_ref, length):
    keys = k_ref.shape[0]
    row = lax.broadcasted_iota(jnp.int32, (keys, LANES), 0)
    lane = lax.broadcasted_iota(jnp.int32, (keys, LANES), 1)
    kaug_ref[:, :LANES] = k_ref[...]
    kaug_ref[:, LANES:] = jnp.where((lane == 0) & (row >= length), MASK_VALUE, 0.0).astype(BF)


def query_with_one(q_half):
    lane = lax.broadcasted_iota(jnp.int32, q_half.shape, 1)
    return jnp.concatenate([q_half, jnp.where(lane == 0, 1.0, 0.0).astype(BF)], axis=1)


def attend_body(len_ref, q_ref, k_ref, v_ref, o_ref, lse_ref, kaug_ref, vt_ref):
    @pl.when(pl.program_id(1) == 0)
    def _():
        key_with_mask(kaug_ref, k_ref, len_ref[0])
        vt_ref[...] = v_ref[...].T

    scaled = q_ref[...] * BF(HD ** (-0.5))
    head = head_of_lane(scaled.shape)
    outs = []
    for h in range(LANES // HD):
        mine = jnp.where(head == h, scaled, BF(0))
        scores = nt(kaug_ref[...], query_with_one(mine))
        row_max = jnp.max(scores, axis=0, keepdims=True)
        exps = jnp.exp(scores - row_max)
        total = jnp.sum(exps, axis=0, keepdims=True)
        probs = (exps * (1.0 / total)).astype(BF)
        outs.append(nn(vt_ref[h * HD : (h + 1) * HD, :], probs))
        lse_ref[0, h : h + 1, :] = row_max + jnp.log(total)
    o_ref[...] = jnp.concatenate(outs, axis=0).T.astype(BF)


def attend(length, qkv, block):
    rows, width = qkv.shape
    pairs = width // 3 // LANES
    return pl.pallas_call(
        attend_body,
        name="attend",
        grid=(pairs, rows // block),
        in_specs=[
            pl.BlockSpec(memory_space=pltpu.SMEM),
            pl.BlockSpec((block, LANES), lambda p, i: (i, p)),
            pl.BlockSpec((rows, LANES), lambda p, i: (0, pairs + p)),
            pl.BlockSpec((rows, LANES), lambda p, i: (0, 2 * pairs + p)),
        ],
        out_specs=[
            pl.BlockSpec((block, LANES), lambda p, i: (i, p)),
            pl.BlockSpec((1, 8, block), lambda p, i: (p, 0, i)),
        ],
        out_shape=[
            jax.ShapeDtypeStruct((rows, width // 3), BF),
            jax.ShapeDtypeStruct((pairs, 8, rows), F32),
        ],
        scratch_shapes=[pltpu.VMEM((rows, 2 * LANES), BF), pltpu.VMEM((LANES, rows), BF)],
        compiler_params=pltpu.CompilerParams(vmem_limit_bytes=VMEM_BYTES),
    )(length, qkv, qkv, qkv)


def turn_back(values, cosine, sine):
    return values * cosine - swap_halves(values) * sine


def attend_grad_body(
    len_ref, q_ref, k_ref, v_ref, g_ref, lse_ref, cosq_ref, sinq_ref, cos_ref, sin_ref,
    dq_ref, dk_ref, dv_ref, bias_ref, kaug_ref, kt_ref, dk_acc, dv_acc,
):
    step = pl.program_id(1)
    scale = HD ** (-0.5)

    @pl.when(step == 0)
    def _():
        key_with_mask(kaug_ref, k_ref, len_ref[0])
        kt_ref[...] = k_ref[...].T
        dk_acc[...] = jnp.zeros_like(dk_acc)
        dv_acc[...] = jnp.zeros_like(dv_acc)
        bias_ref[...] = jnp.zeros_like(bias_ref)

    scaled = q_ref[...] * BF(scale)
    grad = g_ref[...]
    head = head_of_lane(scaled.shape)
    turned, probs_all, scores_all, queries, grads = [], [], [], [], []
    for h in range(LANES // HD):
        mine = jnp.where(head == h, scaled, BF(0))
        my_grad = jnp.where(head == h, grad, BF(0))
        scores = nt(kaug_ref[...], query_with_one(mine))
        probs = jnp.exp(scores - lse_ref[0, h : h + 1, :])
        probs_grad = nt(v_ref[...], my_grad)
        weighted = probs * probs_grad
        row_dot = jnp.sum(weighted, axis=0, keepdims=True)
        scores_grad = (weighted - probs * row_dot).astype(BF)
        turned.append(nn(kt_ref[h * HD : (h + 1) * HD, :], scores_grad))
        probs_all.append(probs.astype(BF))
        scores_all.append(scores_grad)
        queries.append(mine)
        grads.append(my_grad)
    dv_acc[...] += nn(jnp.concatenate(probs_all, axis=1), jnp.concatenate(grads, axis=0))
    dk_acc[...] += nn(jnp.concatenate(scores_all, axis=1), jnp.concatenate(queries, axis=0))
    dq = turn_back((jnp.concatenate(turned, axis=0) * scale).T, cosq_ref[...], sinq_ref[...])
    dq_ref[...] = dq.astype(BF)
    bias_ref[0, 0:1, :] += jnp.sum(dq, axis=0, keepdims=True)

    @pl.when(step == pl.num_programs(1) - 1)
    def _():
        dk = turn_back(dk_acc[...], cos_ref[...], sin_ref[...])
        dk_ref[...] = dk.astype(BF)
        bias_ref[0, 1:2, :] = jnp.sum(dk, axis=0, keepdims=True)
        dv = dv_acc[...]
        dv_ref[...] = dv.astype(BF)
        bias_ref[0, 2:3, :] = jnp.sum(dv, axis=0, keepdims=True)


def attend_grad(length, qkv, grad, lse, cosine, sine, block):
    rows, width = qkv.shape
    pairs = width // 3 // LANES
    whole = pl.BlockSpec((rows, LANES), lambda p, i: (0, p))
    return pl.pallas_call(
        attend_grad_body,
        name="attend_grad",
        grid=(pairs, rows // block),
        in_specs=[
            pl.BlockSpec(memory_space=pltpu.SMEM),
            pl.BlockSpec((block, LANES), lambda p, i: (i, p)),
            pl.BlockSpec((rows, LANES), lambda p, i: (0, pairs + p)),
            pl.BlockSpec((rows, LANES), lambda p, i: (0, 2 * pairs + p)),
            pl.BlockSpec((block, LANES), lambda p, i: (i, p)),
            pl.BlockSpec((1, 8, block), lambda p, i: (p, 0, i)),
            pl.BlockSpec((block, LANES), lambda p, i: (i, 0)),
            pl.BlockSpec((block, LANES), lambda p, i: (i, 0)),
            pl.BlockSpec((rows, LANES), lambda p, i: (0, 0)),
            pl.BlockSpec((rows, LANES), lambda p, i: (0, 0)),
        ],
        out_specs=[
            pl.BlockSpec((block, LANES), lambda p, i: (i, p)),
            whole,
            whole,
            pl.BlockSpec((1, 8, LANES), lambda p, i: (p, 0, 0)),
        ],
        out_shape=[
            jax.ShapeDtypeStruct((rows, width // 3), BF),
            jax.ShapeDtypeStruct((rows, width // 3), BF),
            jax.ShapeDtypeStruct((rows, width // 3), BF),
            jax.ShapeDtypeStruct((pairs, 8, LANES), F32),
        ],
        scratch_shapes=[
            pltpu.VMEM((rows, 2 * LANES), BF),
            pltpu.VMEM((LANES, rows), BF),
            pltpu.VMEM((rows, LANES), F32),
            pltpu.VMEM((rows, LANES), F32),
        ],
        compiler_params=pltpu.CompilerParams(vmem_limit_bytes=VMEM_BYTES),
    )(length, qkv, qkv, qkv, grad, lse, cosine, sine, cosine, sine)


def norm_rows(values):
    mean = jnp.mean(values, axis=-1, keepdims=True)
    centred = values - mean
    inv_std = lax.rsqrt(jnp.mean(centred * centred, axis=-1, keepdims=True) + NORM_EPS)
    return centred * inv_std, inv_std


def norm_rows_grad(upstream, normed, inv_std, gain):
    scaled = upstream * gain
    return inv_std * (
        scaled
        - jnp.mean(scaled, axis=-1, keepdims=True)
        - normed * jnp.mean(scaled * normed, axis=-1, keepdims=True)
    )


def column_sum(values):
    return jnp.sum(values, axis=0, keepdims=True)


OUT_BIAS, GAIN1, SHIFT1, DOWN_BIAS, GAIN2, SHIFT2 = range(6)


def middle_body(
    ctx_ref, tok_ref, cot_ref, out_ref, up_ref, down_ref, vec_ref, upb_ref,
    y_ref, hid_ref, act_ref, g2_ref, gup_ref, g1_ref, g1low_ref, gctx_ref, sums_ref, upsum_ref,
    slope_ref,
):
    @pl.when(pl.program_id(0) == 0)
    def _():
        sums_ref[...] = jnp.zeros_like(sums_ref)
        upsum_ref[...] = jnp.zeros_like(upsum_ref)

    def vec(at):
        return vec_ref[at : at + 1, :]

    parts, _, unit = up_ref.shape
    pre_one = tok_ref[...].astype(F32) + nn(ctx_ref[...], out_ref[...]) + vec(OUT_BIAS)
    normed_one, inv_one = norm_rows(pre_one)
    hidden = normed_one * vec(GAIN1) + vec(SHIFT1)
    hidden_low = hidden.astype(BF)
    hid_ref[...] = hidden_low
    downward = vec(DOWN_BIAS)
    for c in range(parts):
        cols = slice(c * unit, (c + 1) * unit)
        upward = nn(hidden_low, up_ref[c]) + upb_ref[0:1, cols]
        phi_cum = 0.5 * (1.0 + lax.erf(upward * (0.5**0.5)))
        density = jnp.exp(-0.5 * upward * upward) * 0.3989422804014327
        active = (upward * phi_cum).astype(BF)
        slope_ref[:, cols] = phi_cum + upward * density
        act_ref[:, cols] = active
        downward = downward + nn(active, down_ref[c])
    normed_two, inv_two = norm_rows(hidden + downward)
    y_ref[...] = (normed_two * vec(GAIN2) + vec(SHIFT2)).astype(BF)
    cot = cot_ref[...].astype(F32)
    grad_two = norm_rows_grad(cot, normed_two, inv_two, vec(GAIN2))
    grad_two_low = grad_two.astype(BF)
    g2_ref[...] = grad_two_low
    sums_ref[GAIN2 : GAIN2 + 1, :] += column_sum(cot * normed_two)
    sums_ref[SHIFT2 : SHIFT2 + 1, :] += column_sum(cot)
    sums_ref[DOWN_BIAS : DOWN_BIAS + 1, :] += column_sum(grad_two)
    upstream = grad_two
    for c in range(parts):
        cols = slice(c * unit, (c + 1) * unit)
        grad_up = nt(grad_two_low, down_ref[c]) * slope_ref[:, cols]
        upsum_ref[0:1, cols] += column_sum(grad_up)
        grad_up_low = grad_up.astype(BF)
        gup_ref[:, cols] = grad_up_low
        upstream = upstream + nt(grad_up_low, up_ref[c])
    grad_one = norm_rows_grad(upstream, normed_one, inv_one, vec(GAIN1))
    grad_one_low = grad_one.astype(BF)
    g1_ref[...] = grad_one
    g1low_ref[...] = grad_one_low
    sums_ref[GAIN1 : GAIN1 + 1, :] += column_sum(upstream * normed_one)
    sums_ref[SHIFT1 : SHIFT1 + 1, :] += column_sum(upstream)
    sums_ref[OUT_BIAS : OUT_BIAS + 1, :] += column_sum(grad_one)
    gctx_ref[...] = nt(grad_one_low, out_ref[...]).astype(BF)


def middle(context, tokens, cotangent, out_w, up_w, down_w, vectors, up_bias, block):
    rows, features = tokens.shape
    parts, _, unit = up_w.shape
    hidden_units = parts * unit

    def rowed(width):
        return pl.BlockSpec((block, width), lambda i: (i, 0))

    def fixed(*shape):
        return pl.BlockSpec(shape, lambda i: (0,) * len(shape), pipeline_mode=pl.Buffered(1))

    def kept(*shape):
        return pl.BlockSpec(shape, lambda i: (0,) * len(shape))

    narrow_rows = jax.ShapeDtypeStruct((rows, features), BF)
    wide_rows = jax.ShapeDtypeStruct((rows, hidden_units), BF)
    return pl.pallas_call(
        middle_body,
        name="middle",
        grid=(rows // block,),
        in_specs=[
            rowed(features), rowed(features), rowed(features),
            fixed(*out_w.shape), fixed(*up_w.shape), fixed(*down_w.shape),
            fixed(*vectors.shape), fixed(*up_bias.shape),
        ],
        out_specs=[
            rowed(features), rowed(features), rowed(hidden_units), rowed(features),
            rowed(hidden_units), rowed(features), rowed(features), rowed(features),
            kept(8, features), kept(8, hidden_units),
        ],
        out_shape=[
            narrow_rows, narrow_rows, wide_rows, narrow_rows,
            wide_rows, jax.ShapeDtypeStruct((rows, features), F32), narrow_rows, narrow_rows,
            jax.ShapeDtypeStruct((8, features), F32), jax.ShapeDtypeStruct((8, hidden_units), F32),
        ],
        scratch_shapes=[pltpu.VMEM((block, hidden_units), F32)],
        compiler_params=pltpu.CompilerParams(vmem_limit_bytes=VMEM_BYTES),
    )(context, tokens, cotangent, out_w, up_w, down_w, vectors, up_bias)


def gather_rows(shard):
    wide_size = lax.axis_size("wide")
    rows, width = shard.shape
    piece = rows // wide_size
    mine = lax.dynamic_slice_in_dim(shard, lax.axis_index("wide") * piece, piece, 0)
    column = lax.all_gather(mine, "narrow", axis=0)
    both = lax.all_gather(column, "wide", axis=0)
    return both.transpose(1, 0, 2, 3).reshape(-1, rows, width)


def reduce_rows(parts):
    mine = lax.psum_scatter(parts, "wide", scatter_dimension=1, tiled=True)
    mine = lax.psum_scatter(mine, "narrow", scatter_dimension=0, tiled=True)
    return lax.all_gather(mine[0], "wide", axis=0, tiled=True).astype(F32)


def tn(left, right):
    return lax.dot_general(left, right, (((0,), (0,)), ((), ())), preferred_element_type=F32)


def shards(
    tokens, lengths, qkv_weight, qkv_bias, out_weight, out_bias, norm1_gain, norm1_shift,
    up_weight, up_bias, down_weight, down_bias, norm2_gain, norm2_shift, cotangent,
):
    narrow_size = lax.axis_size("narrow")
    at = lax.axis_index("narrow")
    _, capacity, features = tokens.shape
    block = 256 if capacity % 256 == 0 else capacity
    own_tokens = tokens[0]
    length = lax.dynamic_slice_in_dim(lengths[0], at, 1, 0)
    shard_cols = qkv_weight.shape[2]
    unit = up_weight.shape[1]
    cosine, sine = rotary_tables(capacity, HD)

    qkv_t = gather_rows(qkv_weight.reshape(features, 3 * shard_cols).T)
    qkv_t = qkv_t.reshape(narrow_size, 3, shard_cols, features).transpose(1, 0, 2, 3)
    qkv_t = qkv_t.reshape(3 * narrow_size * shard_cols, features)
    biases = lax.all_gather(
        jnp.concatenate([qkv_bias.reshape(-1), up_bias]).astype(F32), "narrow", axis=0
    )
    qkv_b = biases[:, : 3 * shard_cols].reshape(narrow_size, 3, shard_cols).transpose(1, 0, 2)
    qkv_b = qkv_b.reshape(1, -1)
    up_b = biases[:, 3 * shard_cols :].reshape(1, -1)
    out_w = gather_rows(out_weight).reshape(-1, features)
    up_w = gather_rows(up_weight)
    down_w = gather_rows(down_weight)
    vectors = jnp.stack(
        [out_bias, norm1_gain, norm1_shift, down_bias, norm2_gain, norm2_shift, down_bias, down_bias]
    ).astype(F32)

    qkv = qkv_project(own_tokens, qkv_t, qkv_b, cosine, sine, block)
    context, lse = attend(length, qkv, block)
    (
        output, hidden_low, active, grad_two_low, grad_up_low, grad_one, grad_one_low, grad_context,
        sums, up_sums,
    ) = middle(context, own_tokens, cotangent[0], out_w, up_w, down_w, vectors, up_b, block)

    down_parts = tn(active, grad_two_low).astype(BF).reshape(narrow_size, unit, features)
    down_grad = reduce_rows(down_parts)
    up_parts = jnp.stack(
        [tn(hidden_low, grad_up_low[:, c * unit : (c + 1) * unit]).astype(BF) for c in range(narrow_size)]
    )
    up_grad = reduce_rows(up_parts)
    out_parts = tn(context, grad_one_low).astype(BF).reshape(narrow_size, -1, features)
    out_grad = reduce_rows(out_parts)

    dq, dk, dv, bias_sums = attend_grad(length, qkv, grad_context, lse, cosine, sine, block)
    qkv_parts = jnp.stack(
        [tn(piece, own_tokens).astype(BF).reshape(narrow_size, shard_cols, features) for piece in (dq, dk, dv)],
        axis=1,
    ).reshape(narrow_size, 3 * shard_cols, features)
    qkv_grad = reduce_rows(qkv_parts).T.reshape(features, 3, shard_cols)
    input_grad = grad_one
    for j, piece in enumerate((dq, dk, dv)):
        input_grad = input_grad + nn(piece, qkv_t[j * features : (j + 1) * features])

    small = jnp.concatenate(
        [sums[:6].reshape(-1), up_sums[0], bias_sums[:, :3].transpose(1, 0, 2).reshape(-1)]
    )
    small = lax.psum(small, ("wide", "narrow"))
    vec = small[: 6 * features].reshape(6, features)
    up_bias_grad = lax.dynamic_slice_in_dim(small[6 * features :], at * unit, unit, 0)
    bias_grad = small[6 * features + narrow_size * unit :].reshape(3, narrow_size * shard_cols)
    bias_grad = lax.dynamic_slice_in_dim(bias_grad, at * shard_cols, shard_cols, 1)
    return (
        output[None], input_grad[None], qkv_grad, bias_grad, out_grad, vec[OUT_BIAS], vec[GAIN1],
        vec[SHIFT1], up_grad, up_bias_grad, down_grad, vec[DOWN_BIAS], vec[GAIN2], vec[SHIFT2],
    )


def solution(mesh):
    rows = P(("wide", "narrow"), None, None)
    return jax.shard_map(
        shards,
        mesh=mesh,
        in_specs=(
            rows, P("wide", None), P(None, None, "narrow"), P(None, "narrow"), P("narrow", None),
            P(), P(), P(), P(None, "narrow"), P("narrow"), P("narrow", None), P(), P(), P(), rows,
        ),
        out_specs=(
            rows, rows, P(None, None, "narrow"), P(None, "narrow"), P("narrow", None), P(), P(),
            P(), P(None, "narrow"), P("narrow"), P("narrow", None), P(), P(), P(),
        ),
        check_vma=False,
    )
```
